32 devices in a mesh: groups: 2 (over y), blk: 4 (over z), subj: 4 (over x, core).
Axes of the slice: x: 2, y: 2, z: 4, core: 2. Of those that a mesh axis runs over, the one named last changes fastest.
Arguments:
- template_verts: float32 [3, 2048], P(None, ('groups', 'blk')), parts along dimension 1, may hold values from -6 to 6
- template_tris: int32 [3, 2048], P(None, ('groups', 'blk')), parts along dimension 1, may hold values from 0 to 255
- local_pairs: int32 [8, 2], P('blk'), may hold values 0 or 1
- partner_blocks: int32 [4, 8], P(None, 'blk'), may hold values from 0 to 1, as said below
- controls: float32 [3, 8192], replicated, may hold values from -6 to 6
- momenta: float32 [128, 3, 8192], P(('groups', 'subj')), parts along dimension 0, may hold values from -0.06 to 0.06
- target_verts: float32 [128, 3, 1024], P(('groups', 'subj'), None, 'blk'), parts along dimension 0, may hold values from -6 to 6
- target_tris: int32 [128, 3, 1024], P(('groups', 'subj'), None, 'blk'), parts along dimension 0, may hold values from 0 to 255
Outputs:
- template_grad: float32 [3, 2048], P(None, ('groups', 'blk')), parts along dimension 1
- momenta_grad: float32 [128, 3, 8192], P(('groups', 'subj'), None, 'blk'), parts along dimension 0
The draws below stay inside these ranges and needn't reach their ends.
There are 2 independent parts, one for each index of `groups`. The reference program is written for one: setup_inputs(seed, part) draws one part's arguments, and reference() takes and returns one part's arrays. A program takes and returns all parts, laid end to end along the dimension named above; an argument that names none is the same for every part. Nothing has to cross between parts.
Inputs may be any that keep to these rules, and one draw needn't show every extreme that they name: Corner k of template triangle t is template vertex (t // 256) * 256 + template_tris[k, t]; corners of one triangle may coincide. Corner k of triangle t of subject s is its vertex (t // 256) * 256 + target_tris[s, k, t]; corners may coincide. `partner_blocks`: for each r, shard d and its mate shard d XOR 2^(r mod L), the entries of the 2 blocks of d form a permutation of 0 to 1, and those of the mate shard its inverse, so that the pairing of blocks is mutual.
All inputs are finite; a program needn't handle non-finite values. No bound on the sum of `local_pairs` on one device may be relied on, other than what follows from the above.
Results may differ from the reference program's by a relative error of at most 0.0001.
Values sent between devices are 32-bit elements; how exact they have to be, the bound alone decides.
A program may use at most 64 MiB of HBM per device.

```python
import jax
import jax.numpy as jnp
from jax import lax

BLK = 128
BLK_DEV = 2
CTRL = 8192
SHARDS = 4
ELEMS = 256
BLOCKS = 8
VERTS = 1024
SUBJ = 64


def draw_partner_blocks(key, part):
    shards = BLOCKS // BLK_DEV
    bit_count = max(shards.bit_length() - 1, 1)
    rounds = []
    for r in range(4):
        round_key = jax.random.fold_in(key, 100 + r)
        scores = jax.random.randint(round_key, (shards, BLK_DEV), 0, 1 << 20)
        scores = scores * BLK_DEV + jnp.arange(BLK_DEV, dtype=jnp.int32)[None]
        forward = jnp.argsort(scores, axis=1).astype(jnp.int32)
        shard_ids = jnp.arange(shards, dtype=jnp.int32)
        mate_ids = shard_ids ^ 1 << r % bit_count
        lower_ids = jnp.minimum(shard_ids, mate_ids)
        chosen = forward[lower_ids]
        inverse = jnp.argsort(chosen, axis=1).astype(jnp.int32)
        result = jnp.where((shard_ids <= mate_ids)[:, None], chosen, inverse)
        rounds.append(result.reshape(-1))
    return jnp.stack(rounds).astype(jnp.int32)


def set_ends(drawn, own_key, smallest, largest):
    index_at = [jax.random.randint(jax.random.fold_in(own_key, axis), (), 0, length) for axis, length in enumerate(drawn.shape)]
    widest = drawn.shape.index(max(drawn.shape))
    beside = index_at[:widest] + [(index_at[widest] + 1) % drawn.shape[widest]] + index_at[widest + 1:]
    return drawn.at[tuple(index_at)].set(smallest).at[tuple(beside)].set(largest)


def shard_levels(rng, dims, pieces, smallest, largest):
    def one(position, parts):
        heights = jax.random.uniform(jax.random.fold_in(jax.random.fold_in(rng, 6), position), (parts,), jnp.float32, smallest / len(pieces), largest / len(pieces))
        return jnp.repeat(jnp.exp(heights), dims[position] // parts).reshape((-1,) + (1,) * (len(dims) - position - 1))

    factor_of = one(*pieces[0])
    for cut in pieces[1:]:
        factor_of = factor_of * one(*cut)
    return factor_of


def gaussian(rng, dims, scale, bound, cuts=(), held_as=jnp.bfloat16):
    values = scale * jax.random.normal(rng, dims, jnp.float32)
    if cuts:
        values = values * shard_levels(rng, dims, cuts, -0.22, 0.18)
    return jnp.clip(values, -bound, bound).astype(held_as)


def setup_inputs(seed: int = 0, part: int = 0) -> dict:
    streams_of = jax.random.split(jax.random.key(seed), 9)
    part_keys = jax.random.split(jax.random.fold_in(streams_of[8], part), 9)
    template_verts = gaussian(part_keys[0], (3, VERTS), 1.0, 6.0, ((1, 4),), jnp.float32)
    template_tris = set_ends(jax.random.randint(part_keys[1], (3, VERTS), 0, ELEMS), jax.random.fold_in(part_keys[1], 1), 0, ELEMS - 1).astype(jnp.int32)
    local_pairs = set_ends((jax.random.randint(streams_of[2], (BLOCKS, BLK_DEV), 0, 2) < 1).astype(jnp.int32), jax.random.fold_in(streams_of[2], 1), 0, 1)
    partner_blocks = draw_partner_blocks(jax.random.fold_in(streams_of[8], 71), part)
    controls = gaussian(streams_of[4], (3, CTRL), 1.0, 6.0, (), jnp.float32)
    momenta = gaussian(part_keys[5], (SUBJ, 3, CTRL), 0.01, 0.06, ((0, 4),), jnp.float32)
    target_verts = gaussian(part_keys[6], (SUBJ, 3, VERTS), 1.0, 6.0, ((0, 4), (2, 4)), jnp.float32)
    target_tris = set_ends(jax.random.randint(part_keys[7], (SUBJ, 3, VERTS), 0, ELEMS), jax.random.fold_in(part_keys[7], 1), 0, ELEMS - 1).astype(jnp.int32)
    return {"template_verts": template_verts, "template_tris": template_tris, "local_pairs": local_pairs, "partner_blocks": partner_blocks, "controls": controls, "momenta": momenta, "target_verts": target_verts, "target_tris": target_tris}


precise = lax.Precision.HIGHEST
AREA_SQ = 0.25

def kernel_matrix(points, centers):
    sq_dist = jnp.zeros((points.shape[1], centers.shape[1]), jnp.float32)
    for k in range(3):
        offset = points[k][:, None] - centers[k][None, :]
        sq_dist = sq_dist + offset * offset
    return jnp.exp(-sq_dist)

def deform(template, moment, controls):
    kernel_mat = kernel_matrix(template, controls)
    flat_moment = moment.reshape(moment.shape[0] * 3, moment.shape[2])
    velocity = jnp.dot(flat_moment, kernel_mat.T, precision=precise)
    return template[None] + velocity.reshape(moment.shape[0], 3, template.shape[1])

def elements(vertices, triangles):
    corner_a = jnp.take(vertices, triangles[0], axis=-1)
    corner_b = jnp.take(vertices, triangles[1], axis=-1)
    corner_c = jnp.take(vertices, triangles[2], axis=-1)
    center = (corner_a + corner_b + corner_c) / 3.0
    edge_one = corner_b - corner_a
    edge_two = corner_c - corner_a
    normal = 0.5 * jnp.stack([edge_one[..., 1, :] * edge_two[..., 2, :] - edge_one[..., 2, :] * edge_two[..., 1, :], edge_one[..., 2, :] * edge_two[..., 0, :] - edge_one[..., 0, :] * edge_two[..., 2, :], edge_one[..., 0, :] * edge_two[..., 1, :] - edge_one[..., 1, :] * edge_two[..., 0, :]], axis=-2)
    return (center, normal)

def pair_total(p_cen, u_nor, q_cen, w_nor):
    sq_dist = jnp.float32(0.0)
    inner_prod = jnp.float32(0.0)
    for k in range(3):
        offset = p_cen[..., k, :, None] - q_cen[..., k, None, :]
        sq_dist = sq_dist + offset * offset
        inner_prod = inner_prod + u_nor[..., k, :, None] * w_nor[..., k, None, :]
    norm_u = jnp.sqrt(lax.optimization_barrier(jnp.sum(u_nor * u_nor, axis=-2)) + AREA_SQ)
    norm_w = jnp.sqrt(lax.optimization_barrier(jnp.sum(w_nor * w_nor, axis=-2)) + AREA_SQ)
    values = jnp.exp(-sq_dist) * inner_prod * inner_prod / (norm_u[..., :, None] * norm_w[..., None, :])
    return lax.optimization_barrier(jnp.sum(values, axis=(-2, -1)))

def reference(template_verts, template_tris, local_pairs, partner_blocks, controls, momenta, target_verts, target_tris):
    offsets = (jnp.arange(VERTS, dtype=jnp.int32) // ELEMS * ELEMS)[None]
    global_tris = template_tris + offsets
    bit_count = SHARDS.bit_length() - 1
    block_ids = jnp.arange(BLOCKS, dtype=jnp.int32)
    shard_base = block_ids // BLK_DEV * BLK_DEV
    local_ids = shard_base[:, None] + jnp.arange(BLK_DEV, dtype=jnp.int32)[None]
    partner_ids = [(block_ids // BLK_DEV ^ 1 << r % bit_count) * BLK_DEV + partner_blocks[r] for r in range(4)]
    pair_mask = local_pairs.astype(jnp.float32)

    def to_blocks(array_in):
        return array_in.reshape(3, BLOCKS, BLK).transpose(1, 0, 2)

    def subject_energy(vertices, target_v, target_t):
        center, normal = elements(vertices, global_tris)
        centers, normals = (to_blocks(center), to_blocks(normal))
        t_center, t_normal = elements(target_v, target_t + offsets)
        target_c, target_n = (to_blocks(t_center), to_blocks(t_normal))
        local_sum = pair_total(centers[:, None], normals[:, None], centers[local_ids], normals[local_ids])
        energy_sum = jnp.sum(local_sum * pair_mask)
        for r in range(4):
            energy_sum = energy_sum + jnp.sum(pair_total(centers, normals, centers[partner_ids[r]], normals[partner_ids[r]]))
        energy_sum = energy_sum - 2.0 * jnp.sum(pair_total(centers, normals, target_c, target_n))
        return energy_sum / BLK
    checked = jax.checkpoint(subject_energy)

    def total_loss(template, moment):
        deformed = deform(template, moment, controls)
        energies = lax.map(lambda subject_item: checked(subject_item[0], subject_item[1], subject_item[2]), (deformed, target_verts, target_tris))
        return jnp.sum(energies)
    gradients = jax.grad(total_loss, argnums=(0, 1))(template_verts, momenta)
    return (gradients[0] / SUBJ, gradients[1])
```

```python
import functools
import math

import jax
import jax.numpy as jnp
from jax import lax
from jax.experimental import pallas as pl
from jax.experimental.pallas import tpu as pltpu
from jax.sharding import PartitionSpec as P

AREA_SQ = 0.25
SCALE = math.sqrt(math.log2(math.e))
LANES = 128
MESH = pl.DeviceIdType.MESH
f32, bf16 = jnp.float32, jnp.bfloat16
NT = (((1,), (1,)), ((), ()))
NN = (((1,), (0,)), ((), ()))


def split(value):
    high = value.astype(bf16)
    return high, (value - high.astype(f32)).astype(bf16)


def mxu(a, b, dims):
    return lax.dot_general(a, b, dims, preferred_element_type=f32)


def pick_lanes(halves, indices):
    out = []
    for idx in indices:
        low = idx & (LANES - 1)
        value = jnp.take_along_axis(halves[0], low, axis=1, mode="promise_in_bounds")
        for h in range(1, len(halves)):
            other = jnp.take_along_axis(halves[h], low, axis=1, mode="promise_in_bounds")
            value = jnp.where(idx >= h * LANES, other, value)
        out.append(value)
    return out


def cross(a, b):
    return [
        a[1] * b[2] - a[2] * b[1],
        a[2] * b[0] - a[0] * b[2],
        a[0] * b[1] - a[1] * b[0],
    ]


def edges(verts, corner_ids):
    corners = [[pick_lanes(verts[d], corner_ids[k]) for d in range(3)] for k in range(3)]
    pieces = []
    for h in range(len(corner_ids[0])):
        a, b, c = [[corners[k][d][h] for d in range(3)] for k in range(3)]
        center = [(a[d] + b[d] + c[d]) * (1.0 / 3.0) for d in range(3)]
        one = [b[d] - a[d] for d in range(3)]
        two = [c[d] - a[d] for d in range(3)]
        normal = [0.5 * v for v in cross(one, two)]
        pieces.append((center, one, two, normal))
    return pieces


def root_norm(normal):
    return jnp.sqrt(normal[0] * normal[0] + normal[1] * normal[1] + normal[2] * normal[2] + AREA_SQ)


def kernel(
    cfg,
    x_ref, tris_ref, local_ref, partner_ref, ctrl_ref, mom_hbm, tv_hbm, tt_hbm,
    tg_out, mg_hbm,
    mom, tv, tt, xs, xb, csc, khi, klo, vel, own, tgt, mates, acc, geo, hot, cots, chi, mg, tgs,
    mom_sem, t_sem, xs_s, xs_r, pn_s, pn_r, ct_s, ct_r, tg_s, tg_r, out_sem,
):
    n, nsub, subjects, elems, ctrl, cdev, bits, chunk = cfg
    rows = 3 * subjects
    halves = elems // LANES
    groups = subjects // 8
    me = lax.axis_index("blk")
    sub = lax.axis_index("subj")

    loads = [pltpu.make_async_copy(mom_hbm, mom, mom_sem.at[0])]
    tloads = [
        pltpu.make_async_copy(tv_hbm, tv, t_sem.at[0]),
        pltpu.make_async_copy(tt_hbm, tt, t_sem.at[1]),
    ]
    for c in loads + tloads:
        c.start()

    barrier = pltpu.get_barrier_semaphore()
    for o in range(1, n):
        pl.semaphore_signal(barrier, inc=1, device_id={"blk": me ^ o}, device_id_type=MESH)
    for o in range(1, nsub):
        pl.semaphore_signal(
            barrier, inc=1, device_id={"subj": lax.rem(sub + o, nsub)}, device_id_type=MESH
        )

    def spread(points, slot):
        padded = jnp.concatenate([points * SCALE, jnp.zeros((5, elems), f32)], axis=0)
        columns = padded.T
        for d in range(3):
            xb[slot, d] = jnp.broadcast_to(columns[:, d : d + 1], (elems, LANES))

    spread(x_ref[...], 0)
    csc[...] = ctrl_ref[...] * SCALE
    vel[...] = jnp.zeros_like(vel)

    def kernel_chunk(slot, start):
        cs = [csc[d : d + 1, pl.ds(start, chunk)] for d in range(3)]
        step = 32
        for r in range(0, elems, step):
            total = None
            for d in range(3):
                xv = xb[slot, d, pl.ds(r, step), :]
                off = jnp.concatenate([xv] * (chunk // LANES), axis=1) - cs[d]
                total = off * off if total is None else total + off * off
            hi, lo = split(jnp.exp2(-total))
            khi[pl.ds(r, step), :] = hi
            klo[pl.ds(r, step), :] = lo

    for c in loads:
        c.wait()

    def forward(i, carry):
        start = pl.multiple_of(i * chunk, chunk)
        kernel_chunk(0, start)
        m = mom[:, pl.ds(start, chunk)]
        weighted = [m]
        for d in range(3):
            weighted.append(m * ctrl_ref[d : d + 1, pl.ds(start, chunk)])
        pairs = [split(w) for w in weighted]
        hi = jnp.concatenate([p[0] for p in pairs], axis=0)
        lo = jnp.concatenate([p[1] for p in pairs], axis=0)
        vel[...] += mxu(hi, khi[...], NT) + mxu(lo, khi[...], NT) + mxu(hi, klo[...], NT)
        return carry

    lax.fori_loop(0, ctrl // chunk, forward, 0)

    pl.semaphore_wait(barrier, n - 1 + nsub - 1)

    def to_blk(src, dst, ssem, rsem, o, s):
        return pltpu.make_async_remote_copy(
            src_ref=src, dst_ref=dst, send_sem=ssem.at[s], recv_sem=rsem.at[s],
            device_id={"blk": me ^ o}, device_id_type=MESH,
        )

    x_sends = [to_blk(x_ref, xs.at[o - 1], xs_s, xs_r, o, o - 1) for o in range(1, n)]
    for c in x_sends:
        c.start()

    lane = lambda h: slice(h * LANES, (h + 1) * LANES)
    for g in range(groups):
        verts = [
            [
                x_ref[d : d + 1, lane(h)] + vel[pl.ds(d * subjects + g * 8, 8), lane(h)]
                for h in range(halves)
            ]
            for d in range(3)
        ]
        ids = [
            [jnp.broadcast_to(tris_ref[k : k + 1, lane(h)], (8, LANES)) for h in range(halves)]
            for k in range(3)
        ]
        for h, (center, one, two, normal) in enumerate(edges(verts, ids)):
            nu = root_norm(normal)
            inv = 1.0 / jnp.sqrt(nu)
            for d in range(3):
                own[d, g, h] = center[d] * SCALE
                own[3 + d, g, h] = normal[d] * inv
                geo[d, g, h] = one[d]
                geo[3 + d, g, h] = two[d]
                geo[6 + d, g, h] = normal[d]
            geo[9, g, h] = nu

    p_sends = [to_blk(own, mates.at[b], pn_s, pn_r, 2**b, b) for b in range(bits)]
    for c in p_sends:
        c.start()

    for c in tloads:
        c.wait()
    for g in range(groups):
        part = lambda d: pl.ds(d * subjects + g * 8, 8)
        verts = [[tv[part(d), lane(h)] for h in range(halves)] for d in range(3)]
        ids = [[tt[part(k), lane(h)] for h in range(halves)] for k in range(3)]
        for h, (center, one, two, normal) in enumerate(edges(verts, ids)):
            inv = 1.0 / jnp.sqrt(root_norm(normal))
            for d in range(3):
                tgt[d, g, h] = center[d] * SCALE
                tgt[3 + d, g, h] = normal[d] * inv

    for k in range(3):
        vertex = lax.broadcasted_iota(jnp.int32, (elems, elems), 0)
        hot[:, k * elems : (k + 1) * elems] = jnp.where(
            vertex == tris_ref[k : k + 1, :], 1.0, 0.0
        ).astype(bf16)

    acc[...] = jnp.zeros_like(acc)

    def interact(load, g, a_blocks, coefs):
        q = load()
        p = [[own[d, g, a] for d in range(3)] for a in a_blocks]
        u = [[geo[6 + d, g, a] for d in range(3)] for a in a_blocks]
        unroll = 4

        def body(i, sums):
            sums = list(sums)
            for v in range(unroll):
                shift = i * unroll + v
                rolled = [pltpu.roll(value, shift, 1) for value in q]
                for x in range(len(a_blocks)):
                    off = [p[x][d] - rolled[d] for d in range(3)]
                    weight = jnp.exp2(-(off[0] * off[0] + off[1] * off[1] + off[2] * off[2]))
                    inner = (
                        u[x][0] * rolled[3] + u[x][1] * rolled[4] + u[x][2] * rolled[5]
                    )
                    t = weight * inner
                    s = t * inner
                    for d in range(3):
                        sums[6 * x + d] = sums[6 * x + d] + s * off[d]
                        sums[6 * x + 3 + d] = sums[6 * x + 3 + d] + t * rolled[3 + d]
            return tuple(sums)

        zero = jnp.zeros((8, LANES), f32)
        sums = lax.fori_loop(0, LANES // unroll, body, (zero,) * (6 * len(a_blocks)))
        for x, a in enumerate(a_blocks):
            for d in range(6):
                acc[d, g, a] += coefs[x] * sums[6 * x + d]

    every = list(range(halves))
    as_float = lambda v: v.astype(f32)
    for b in range(halves):
        local = [as_float(local_ref[a, b] + local_ref[b, a]) for a in every]

        def near(g, carry, b=b, local=local):
            interact(lambda: [tgt[d, g, b] for d in range(6)], g, [b], [-2.0])
            interact(lambda: [own[d, g, b] for d in range(6)], g, every, local)
            return carry

        lax.fori_loop(0, groups, near, 0)

    for bit in range(bits):
        p_sends[bit].wait_recv()
        for b in range(halves):
            coefs = []
            for a in every:
                count = jnp.int32(0)
                for r in range(4):
                    if r % (n.bit_length() - 1) == bit:
                        count = count + jnp.where(partner_ref[r, a] == b, 2, 0)
                coefs.append(as_float(count))

            def far(g, carry, b=b, bit=bit, coefs=coefs):
                interact(lambda: [mates[bit, d, g, b] for d in range(6)], g, every, coefs)
                return carry

            lax.fori_loop(0, groups, far, 0)

    width = 1.0 / LANES
    corner = [[[[None] * halves for _ in range(groups)] for _ in range(3)] for _ in range(3)]
    for g in range(groups):
        for h in range(halves):
            one = [geo[d, g, h] for d in range(3)]
            two = [geo[3 + d, g, h] for d in range(3)]
            u = [geo[6 + d, g, h] for d in range(3)]
            inv = 1.0 / geo[9, g, h]
            moved = [acc[d, g, h] for d in range(3)]
            turned = [acc[3 + d, g, h] for d in range(3)]
            total = u[0] * turned[0] + u[1] * turned[1] + u[2] * turned[2]
            shrink = inv * inv * inv * total
            gp = [moved[d] * inv * (-2.0 * width / SCALE / 3.0) for d in range(3)]
            gu = [(2.0 * inv * turned[d] - u[d] * shrink) * (0.5 * width) for d in range(3)]
            g_one = cross(two, gu)
            g_two = cross(gu, one)
            for d in range(3):
                corner[0][d][g][h] = gp[d] - g_one[d] - g_two[d]
                corner[1][d][g][h] = gp[d] + g_one[d]
                corner[2][d][g][h] = gp[d] + g_two[d]
    for k in range(3):
        for h in range(halves):
            column = pl.ds(k * elems + h * LANES, LANES)
            value = jnp.concatenate(
                [corner[k][d][g][h] for d in range(3) for g in range(groups)], axis=0
            )
            hi, lo = split(value)
            chi[0:rows, column] = hi
            chi[rows : 2 * rows, column] = lo
    both = mxu(chi[...], hot[...], NT)
    cot = both[0:rows] + both[rows : 2 * rows]
    cots[0] = cot

    c_sends = [to_blk(cots.at[0], cots.at[o], ct_s, ct_r, o, o - 1) for o in range(1, n)]
    for c in c_sends:
        c.start()

    def over_rows(value):
        return jnp.sum(value, axis=0, keepdims=True)

    plain = over_rows(cot * vel[0:rows, :])
    factor = 1.0 / (subjects * nsub)
    for d in range(3):
        direct = over_rows(cot[d * subjects : (d + 1) * subjects])
        moved = over_rows(cot * vel[(d + 1) * rows : (d + 2) * rows, :])
        tgs[sub, pl.ds(d, 1), :] = factor * (direct - 2.0 * (x_ref[d : d + 1, :] * plain - moved))

    g_sends = []
    for o in range(1, nsub):
        g_sends.append(
            pltpu.make_async_remote_copy(
                src_ref=tgs.at[sub], dst_ref=tgs.at[sub], send_sem=tg_s.at[o - 1],
                recv_sem=tg_r.at[o - 1], device_id={"subj": lax.rem(sub + o, nsub)},
                device_id_type=MESH,
            )
        )
    for c in g_sends:
        c.start()

    for o in range(1, n):
        x_sends[o - 1].wait_recv()
        spread(xs[o - 1], o)

    for o in range(n):
        if o:
            c_sends[o - 1].wait_recv()
        hi, lo = split(cots[o])

        def backward(i, carry, o=o, hi=hi, lo=lo):
            start = pl.multiple_of(i * chunk, chunk)
            kernel_chunk(o, pl.multiple_of(me * cdev + i * chunk, chunk))
            term = mxu(hi, khi[...], NN) + mxu(lo, khi[...], NN) + mxu(hi, klo[...], NN)
            if o:
                mg[:, pl.ds(start, chunk)] += term
            else:
                mg[:, pl.ds(start, chunk)] = term
            return carry

        lax.fori_loop(0, cdev // chunk, backward, 0)

    outs = [pltpu.make_async_copy(mg, mg_hbm, out_sem.at[0])]
    for c in outs:
        c.start()
    for c in g_sends:
        c.wait_recv()
    tg_sum = tgs[0]
    for o in range(1, nsub):
        tg_sum = tg_sum + tgs[o]
    tg_out[...] = tg_sum
    for c in x_sends + p_sends + c_sends + g_sends:
        c.wait_send()
    for c in outs:
        c.wait()


def on_device(n, nsub, tverts, ttris, local, partner, controls, momenta, tv, tt):
    subjects, _, ctrl = momenta.shape
    elems = tverts.shape[1]
    halves = elems // LANES
    groups = subjects // 8
    rows = 3 * subjects
    cdev = ctrl // n
    bits = min(4, n.bit_length() - 1)
    chunk = min(512, cdev)
    cfg = (n, nsub, subjects, elems, ctrl, cdev, bits, chunk)
    vmem = pl.BlockSpec(memory_space=pltpu.VMEM)
    smem = pl.BlockSpec(memory_space=pltpu.SMEM)
    hbm = pl.BlockSpec(memory_space=pl.ANY)
    panel = (6, groups, halves, 8, LANES)
    dma = pltpu.SemaphoreType.DMA
    by_axis = lambda v: v.transpose(1, 0, 2).reshape(rows, v.shape[2])
    template_grad, grads = pl.pallas_call(
        functools.partial(kernel, cfg),
        out_shape=(
            jax.ShapeDtypeStruct((3, elems), f32),
            jax.ShapeDtypeStruct((rows, cdev), f32),
        ),
        in_specs=[vmem, vmem, smem, smem, vmem, hbm, hbm, hbm],
        out_specs=(vmem, hbm),
        scratch_shapes=[
            pltpu.VMEM((rows, ctrl), f32),
            pltpu.VMEM((rows, elems), f32),
            pltpu.VMEM((rows, elems), jnp.int32),
            pltpu.VMEM((n - 1, 3, elems), f32),
            pltpu.VMEM((n, 3, elems, LANES), f32),
            pltpu.VMEM((3, ctrl), f32),
            pltpu.VMEM((elems, chunk), bf16),
            pltpu.VMEM((elems, chunk), bf16),
            pltpu.VMEM((4 * rows, elems), f32),
            pltpu.VMEM(panel, f32),
            pltpu.VMEM(panel, f32),
            pltpu.VMEM((bits,) + panel, f32),
            pltpu.VMEM(panel, f32),
            pltpu.VMEM((10,) + panel[1:], f32),
            pltpu.VMEM((elems, 3 * elems), bf16),
            pltpu.VMEM((n, rows, elems), f32),
            pltpu.VMEM((2 * rows, 3 * elems), bf16),
            pltpu.VMEM((rows, cdev), f32),
            pltpu.VMEM((nsub, 3, elems), f32),
            dma((1,)), dma((2,)),
            dma((n - 1,)), dma((n - 1,)),
            dma((bits,)), dma((bits,)),
            dma((n - 1,)), dma((n - 1,)),
            dma((nsub - 1,)), dma((nsub - 1,)),
            dma((1,)),
        ],
        compiler_params=pltpu.CompilerParams(
            collective_id=0, has_side_effects=True, vmem_limit_bytes=48 * 2**20
        ),
        name="atlas",
    )(tverts, ttris, local, partner, controls, by_axis(momenta), by_axis(tv), by_axis(tt))
    return template_grad, grads.reshape(3, subjects, cdev).transpose(1, 0, 2)


def solution(mesh):
    return jax.shard_map(
        functools.partial(on_device, mesh.shape["blk"], mesh.shape["subj"]),
        mesh=mesh,
        in_specs=(
            P(None, ("groups", "blk")),
            P(None, ("groups", "blk")),
            P("blk", None),
            P(None, "blk"),
            P(),
            P(("groups", "subj"), None, None),
            P(("groups", "subj"), None, "blk"),
            P(("groups", "subj"), None, "blk"),
        ),
        out_specs=(P(None, ("groups", "blk")), P(("groups", "subj"), None, "blk")),
        check_vma=False,
    )
```

```python
import functools
import math

import jax
import jax.numpy as jnp
from jax import lax
from jax.experimental import pallas as pl
from jax.experimental.pallas import tpu as pltpu
from jax.sharding import PartitionSpec as P

AREA_SQ = 0.25
SCALE = math.sqrt(math.log2(math.e))
LANES = 128
UNROLL = 64
MESH = pl.DeviceIdType.MESH
f32, bf16 = jnp.float32, jnp.bfloat16
NT = (((1,), (1,)), ((), ()))
NN = (((1,), (0,)), ((), ()))


def split(value):
    high = value.astype(bf16)
    return high, (value - high.astype(f32)).astype(bf16)


def mxu(a, b, dims):
    return lax.dot_general(a, b, dims, preferred_element_type=f32)


def pick_lanes(halves, indices):
    out = []
    for idx in indices:
        low = idx & (LANES - 1)
        value = jnp.take_along_axis(halves[0], low, axis=1, mode="promise_in_bounds")
        for h in range(1, len(halves)):
            other = jnp.take_along_axis(halves[h], low, axis=1, mode="promise_in_bounds")
            value = jnp.where(idx >= h * LANES, other, value)
        out.append(value)
    return out


def cross(a, b):
    return [
        a[1] * b[2] - a[2] * b[1],
        a[2] * b[0] - a[0] * b[2],
        a[0] * b[1] - a[1] * b[0],
    ]


def edges(verts, corner_ids):
    corners = [[pick_lanes(verts[d], corner_ids[k]) for d in range(3)] for k in range(3)]
    pieces = []
    for h in range(len(corner_ids[0])):
        a, b, c = [[corners[k][d][h] for d in range(3)] for k in range(3)]
        center = [(a[d] + b[d] + c[d]) * (1.0 / 3.0) for d in range(3)]
        one = [b[d] - a[d] for d in range(3)]
        two = [c[d] - a[d] for d in range(3)]
        normal = [0.5 * v for v in cross(one, two)]
        pieces.append((center, one, two, normal))
    return pieces


def root_norm(normal):
    return jnp.sqrt(normal[0] * normal[0] + normal[1] * normal[1] + normal[2] * normal[2] + AREA_SQ)


def kernel(
    cfg,
    x_hbm, tris_hbm, local_hbm, partner_hbm, ctrl_hbm, mom_hbm, tv_hbm, tt_hbm,
    tg_out, mg_hbm,
    x_ref, tris_ref, local_ref, partner_ref, ctrl_ref, mom, tv, tt, xs, xb, csc, khi, klo, vel, own, tgt, mates, acc, geo, hot, cots, chi, mg, tgs,
    mom_sem, t_sem, xs_s, xs_r, pn_s, pn_r, ct_s, ct_r, tg_s, tg_r, out_sem,
):
    n, nsub, subjects, elems, ctrl, cdev, bits, chunk = cfg
    rows = 3 * subjects
    halves = elems // LANES
    groups = subjects // 8
    me = lax.axis_index("blk")
    sub = lax.axis_index("subj")

    loads = [
        pltpu.make_async_copy(x_hbm, x_ref, mom_sem.at[0]),
        pltpu.make_async_copy(ctrl_hbm, ctrl_ref, mom_sem.at[1]),
        pltpu.make_async_copy(mom_hbm, mom, mom_sem.at[2]),
    ]
    tloads = [
        pltpu.make_async_copy(tris_hbm, tris_ref, t_sem.at[0]),
        pltpu.make_async_copy(tv_hbm, tv, t_sem.at[1]),
        pltpu.make_async_copy(tt_hbm, tt, t_sem.at[2]),
        pltpu.make_async_copy(local_hbm, local_ref, t_sem.at[3]),
        pltpu.make_async_copy(partner_hbm, partner_ref, t_sem.at[4]),
    ]
    for c in loads + tloads:
        c.start()

    barrier = pltpu.get_barrier_semaphore()
    for o in range(1, n):
        pl.semaphore_signal(barrier, inc=1, device_id={"blk": me ^ o}, device_id_type=MESH)
    for o in range(1, nsub):
        pl.semaphore_signal(
            barrier, inc=1, device_id={"subj": lax.rem(sub + o, nsub)}, device_id_type=MESH
        )

    def spread(points, slot):
        padded = jnp.concatenate([points * SCALE, jnp.zeros((5, elems), f32)], axis=0)
        columns = padded.T
        for d in range(3):
            xb[slot, d] = jnp.broadcast_to(columns[:, d : d + 1], (elems, LANES))

    loads[0].wait()
    spread(x_ref[...], 0)
    loads[1].wait()
    csc[...] = ctrl_ref[...] * SCALE
    vel[...] = jnp.zeros_like(vel)

    def kernel_chunk(slot, start):
        cs = [csc[d : d + 1, pl.ds(start, chunk)] for d in range(3)]
        step = 32
        for r in range(0, elems, step):
            total = None
            for d in range(3):
                xv = xb[slot, d, pl.ds(r, step), :]
                off = jnp.concatenate([xv] * (chunk // LANES), axis=1) - cs[d]
                total = off * off if total is None else total + off * off
            hi, lo = split(jnp.exp2(-total))
            khi[pl.ds(r, step), :] = hi
            klo[pl.ds(r, step), :] = lo

    loads[2].wait()

    def forward(i, carry):
        start = pl.multiple_of(i * chunk, chunk)
        kernel_chunk(0, start)
        m = mom[:, pl.ds(start, chunk)]
        weighted = [m]
        for d in range(3):
            weighted.append(m * ctrl_ref[d : d + 1, pl.ds(start, chunk)])
        pairs = [split(w) for w in weighted]
        hi = jnp.concatenate([p[0] for p in pairs], axis=0)
        lo = jnp.concatenate([p[1] for p in pairs], axis=0)
        vel[...] += mxu(hi, khi[...], NT) + mxu(lo, khi[...], NT) + mxu(hi, klo[...], NT)
        return carry

    lax.fori_loop(0, ctrl // chunk, forward, 0)

    pl.semaphore_wait(barrier, n - 1 + nsub - 1)

    def to_blk(src, dst, ssem, rsem, o, s):
        return pltpu.make_async_remote_copy(
            src_ref=src, dst_ref=dst, send_sem=ssem.at[s], recv_sem=rsem.at[s],
            device_id={"blk": me ^ o}, device_id_type=MESH,
        )

    x_sends = [to_blk(x_ref, xs.at[o - 1], xs_s, xs_r, o, o - 1) for o in range(1, n)]
    for c in x_sends:
        c.start()

    tloads[0].wait()
    lane = lambda h: slice(h * LANES, (h + 1) * LANES)
    for g in range(groups):
        verts = [
            [
                x_ref[d : d + 1, lane(h)] + vel[pl.ds(d * subjects + g * 8, 8), lane(h)]
                for h in range(halves)
            ]
            for d in range(3)
        ]
        ids = [
            [jnp.broadcast_to(tris_ref[k : k + 1, lane(h)], (8, LANES)) for h in range(halves)]
            for k in range(3)
        ]
        for h, (center, one, two, normal) in enumerate(edges(verts, ids)):
            nu = root_norm(normal)
            inv = 1.0 / jnp.sqrt(nu)
            for d in range(3):
                own[d, g, h] = center[d] * SCALE
                own[3 + d, g, h] = normal[d] * inv
                geo[d, g, h] = one[d]
                geo[3 + d, g, h] = two[d]
                geo[6 + d, g, h] = normal[d]
            geo[9, g, h] = nu

    p_sends = [to_blk(own, mates.at[b], pn_s, pn_r, 2**b, b) for b in range(bits)]
    for c in p_sends:
        c.start()

    for c in tloads[1:]:
        c.wait()
    for g in range(groups):
        part = lambda d: pl.ds(d * subjects + g * 8, 8)
        verts = [[tv[part(d), lane(h)] for h in range(halves)] for d in range(3)]
        ids = [[tt[part(k), lane(h)] for h in range(halves)] for k in range(3)]
        for h, (center, one, two, normal) in enumerate(edges(verts, ids)):
            inv = 1.0 / jnp.sqrt(root_norm(normal))
            for d in range(3):
                tgt[d, g, h] = center[d] * SCALE
                tgt[3 + d, g, h] = normal[d] * inv

    for k in range(3):
        vertex = lax.broadcasted_iota(jnp.int32, (elems, elems), 0)
        hot[:, k * elems : (k + 1) * elems] = jnp.where(
            vertex == tris_ref[k : k + 1, :], 1.0, 0.0
        ).astype(bf16)

    acc[...] = jnp.zeros_like(acc)

    def interact(q, g, a_blocks, coefs):
        p = [[own[d, g, a] for d in range(3)] for a in a_blocks]
        u = [[geo[6 + d, g, a] for d in range(3)] for a in a_blocks]
        unroll = UNROLL

        def body(i, sums):
            sums = list(sums)
            for v in range(unroll):
                shift = v if unroll == LANES else i * unroll + v
                rolled = [pltpu.roll(value, shift, 1) if v or unroll < LANES else value for value in q]
                for x in range(len(a_blocks)):
                    off = [p[x][d] - rolled[d] for d in range(3)]
                    weight = jnp.exp2(-(off[0] * off[0] + off[1] * off[1] + off[2] * off[2]))
                    inner = (
                        u[x][0] * rolled[3] + u[x][1] * rolled[4] + u[x][2] * rolled[5]
                    )
                    t = weight * inner
                    s = t * inner
                    for d in range(3):
                        sums[6 * x + d] = sums[6 * x + d] + s * off[d]
                        sums[6 * x + 3 + d] = sums[6 * x + 3 + d] + t * rolled[3 + d]
            return tuple(sums)

        sums = (jnp.zeros((8, LANES), f32),) * (6 * len(a_blocks))
        if unroll == LANES:
            sums = body(0, sums)
        else:
            sums = lax.fori_loop(0, LANES // unroll, body, sums)
        for x, a in enumerate(a_blocks):
            for d in range(6):
                acc[d, g, a] += coefs[x] * sums[6 * x + d]

    every = list(range(halves))
    as_float = lambda v: v.astype(f32)

    def near_target(i, carry):
        b, g = i // groups, i % groups
        interact([tgt[d, g, b] for d in range(6)], g, [b], [-2.0])
        return carry

    def near_own(i, carry):
        b, g = i // groups, i % groups
        local = [as_float(local_ref[a, b] + local_ref[b, a]) for a in every]
        interact([own[d, g, b] for d in range(6)], g, every, local)
        return carry

    lax.fori_loop(0, halves * groups, near_target, 0)
    lax.fori_loop(0, halves * groups, near_own, 0)

    for bit in range(bits):
        p_sends[bit].wait_recv()

        def far(i, carry, bit=bit):
            b, g = i // groups, i % groups
            coefs = []
            for a in every:
                count = jnp.int32(0)
                for r in range(4):
                    if r % (n.bit_length() - 1) == bit:
                        count = count + jnp.where(partner_ref[a, r] == b, 2, 0)
                coefs.append(as_float(count))
            interact([mates[bit, d, g, b] for d in range(6)], g, every, coefs)
            return carry

        lax.fori_loop(0, halves * groups, far, 0)

    width = 1.0 / LANES
    corner = [[[[None] * halves for _ in range(groups)] for _ in range(3)] for _ in range(3)]
    for g in range(groups):
        for h in range(halves):
            one = [geo[d, g, h] for d in range(3)]
            two = [geo[3 + d, g, h] for d in range(3)]
            u = [geo[6 + d, g, h] for d in range(3)]
            inv = 1.0 / geo[9, g, h]
            moved = [acc[d, g, h] for d in range(3)]
            turned = [acc[3 + d, g, h] for d in range(3)]
            total = u[0] * turned[0] + u[1] * turned[1] + u[2] * turned[2]
            shrink = inv * inv * inv * total
            gp = [moved[d] * inv * (-2.0 * width / SCALE / 3.0) for d in range(3)]
            gu = [(2.0 * inv * turned[d] - u[d] * shrink) * (0.5 * width) for d in range(3)]
            g_one = cross(two, gu)
            g_two = cross(gu, one)
            for d in range(3):
                corner[0][d][g][h] = gp[d] - g_one[d] - g_two[d]
                corner[1][d][g][h] = gp[d] + g_one[d]
                corner[2][d][g][h] = gp[d] + g_two[d]
    for k in range(3):
        for h in range(halves):
            column = pl.ds(k * elems + h * LANES, LANES)
            value = jnp.concatenate(
                [corner[k][d][g][h] for d in range(3) for g in range(groups)], axis=0
            )
            hi, lo = split(value)
            chi[0:rows, column] = hi
            chi[rows : 2 * rows, column] = lo
    both = mxu(chi[...], hot[...], NT)
    cot = both[0:rows] + both[rows : 2 * rows]
    cots[0] = cot

    c_sends = [to_blk(cots.at[0], cots.at[o], ct_s, ct_r, o, o - 1) for o in range(1, n)]
    for c in c_sends:
        c.start()

    def over_rows(value):
        return jnp.sum(value, axis=0, keepdims=True)

    plain = over_rows(cot * vel[0:rows, :])
    factor = 1.0 / (subjects * nsub)
    for d in range(3):
        direct = over_rows(cot[d * subjects : (d + 1) * subjects])
        moved = over_rows(cot * vel[(d + 1) * rows : (d + 2) * rows, :])
        tgs[sub, pl.ds(d, 1), :] = factor * (direct - 2.0 * (x_ref[d : d + 1, :] * plain - moved))

    g_sends = []
    for o in range(1, nsub):
        g_sends.append(
            pltpu.make_async_remote_copy(
                src_ref=tgs.at[sub], dst_ref=tgs.at[sub], send_sem=tg_s.at[o - 1],
                recv_sem=tg_r.at[o - 1], device_id={"subj": lax.rem(sub + o, nsub)},
                device_id_type=MESH,
            )
        )
    for c in g_sends:
        c.start()

    for o in range(1, n):
        x_sends[o - 1].wait_recv()
        spread(xs[o - 1], o)

    for o in range(n):
        if o:
            c_sends[o - 1].wait_recv()
        hi, lo = split(cots[o])

        def backward(i, carry, o=o, hi=hi, lo=lo):
            start = pl.multiple_of(i * chunk, chunk)
            kernel_chunk(o, pl.multiple_of(me * cdev + i * chunk, chunk))
            term = mxu(hi, khi[...], NN) + mxu(lo, khi[...], NN) + mxu(hi, klo[...], NN)
            if o:
                mg[:, pl.ds(start, chunk)] += term
            else:
                mg[:, pl.ds(start, chunk)] = term
            return carry

        lax.fori_loop(0, cdev // chunk, backward, 0)

    outs = [pltpu.make_async_copy(mg, mg_hbm, out_sem.at[0])]
    for c in outs:
        c.start()
    for c in g_sends:
        c.wait_recv()
    tg_sum = tgs[0]
    for o in range(1, nsub):
        tg_sum = tg_sum + tgs[o]
    tg_out[...] = tg_sum
    for c in x_sends + p_sends + c_sends + g_sends:
        c.wait_send()
    for c in outs:
        c.wait()


def on_device(n, nsub, tverts, ttris, local, partner, controls, momenta, tv, tt):
    subjects, _, ctrl = momenta.shape
    elems = tverts.shape[1]
    halves = elems // LANES
    groups = subjects // 8
    rows = 3 * subjects
    cdev = ctrl // n
    bits = min(4, n.bit_length() - 1)
    chunk = min(512, cdev)
    cfg = (n, nsub, subjects, elems, ctrl, cdev, bits, chunk)
    vmem = pl.BlockSpec(memory_space=pltpu.VMEM)
    hbm = pl.BlockSpec(memory_space=pltpu.HBM)
    panel = (6, groups, halves, 8, LANES)
    dma = pltpu.SemaphoreType.DMA
    by_axis = lambda v: v.transpose(1, 0, 2).reshape(rows, v.shape[2])
    template_grad, grads = pl.pallas_call(
        functools.partial(kernel, cfg),
        out_shape=(
            jax.ShapeDtypeStruct((3, elems), f32),
            jax.ShapeDtypeStruct((rows, cdev), f32),
        ),
        in_specs=[hbm] * 8,
        out_specs=(vmem, hbm),
        scratch_shapes=[
            pltpu.VMEM((3, elems), f32),
            pltpu.VMEM((3, elems), jnp.int32),
            pltpu.SMEM(local.shape, jnp.int32),
            pltpu.SMEM(partner.shape[::-1], jnp.int32),
            pltpu.VMEM((3, ctrl), f32),
            pltpu.VMEM((rows, ctrl), f32),
            pltpu.VMEM((rows, elems), f32),
            pltpu.VMEM((rows, elems), jnp.int32),
            pltpu.VMEM((n - 1, 3, elems), f32),
            pltpu.VMEM((n, 3, elems, LANES), f32),
            pltpu.VMEM((3, ctrl), f32),
            pltpu.VMEM((elems, chunk), bf16),
            pltpu.VMEM((elems, chunk), bf16),
            pltpu.VMEM((4 * rows, elems), f32),
            pltpu.VMEM(panel, f32),
            pltpu.VMEM(panel, f32),
            pltpu.VMEM((bits,) + panel, f32),
            pltpu.VMEM(panel, f32),
            pltpu.VMEM((10,) + panel[1:], f32),
            pltpu.VMEM((elems, 3 * elems), bf16),
            pltpu.VMEM((n, rows, elems), f32),
            pltpu.VMEM((2 * rows, 3 * elems), bf16),
            pltpu.VMEM((rows, cdev), f32),
            pltpu.VMEM((nsub, 3, elems), f32),
            dma((3,)), dma((5,)),
            dma((n - 1,)), dma((n - 1,)),
            dma((bits,)), dma((bits,)),
            dma((n - 1,)), dma((n - 1,)),
            dma((nsub - 1,)), dma((nsub - 1,)),
            dma((1,)),
        ],
        compiler_params=pltpu.CompilerParams(
            collective_id=0, has_side_effects=True, vmem_limit_bytes=64 * 2**20
        ),
        name="atlas",
    )(tverts, ttris, local, partner.T, controls, by_axis(momenta), by_axis(tv), by_axis(tt))
    return template_grad, grads.reshape(3, subjects, cdev).transpose(1, 0, 2)


def solution(mesh):
    return jax.shard_map(
        functools.partial(on_device, mesh.shape["blk"], mesh.shape["subj"]),
        mesh=mesh,
        in_specs=(
            P(None, ("groups", "blk")),
            P(None, ("groups", "blk")),
            P("blk", None),
            P(None, "blk"),
            P(),
            P(("groups", "subj"), None, None),
            P(("groups", "subj"), None, "blk"),
            P(("groups", "subj"), None, "blk"),
        ),
        out_specs=(P(None, ("groups", "blk")), P(("groups", "subj"), None, "blk")),
        check_vma=False,
    )
```

```python
import functools
import math

import jax
import jax.numpy as jnp
from jax import lax
from jax.experimental import pallas as pl
from jax.experimental.pallas import tpu as pltpu
from jax.sharding import PartitionSpec as P

AREA_SQ = 0.25
SCALE = math.sqrt(math.log2(math.e))
LANES = 128
UNROLL = 64
MESH = pl.DeviceIdType.MESH
f32, bf16 = jnp.float32, jnp.bfloat16
NT = (((1,), (1,)), ((), ()))
NN = (((1,), (0,)), ((), ()))


def split(value):
    high = value.astype(bf16)
    return high, (value - high.astype(f32)).astype(bf16)


def mxu(a, b, dims):
    return lax.dot_general(a, b, dims, preferred_element_type=f32)


def pick_lanes(halves, indices):
    out = []
    for idx in indices:
        low = idx & (LANES - 1)
        value = jnp.take_along_axis(halves[0], low, axis=1, mode="promise_in_bounds")
        for h in range(1, len(halves)):
            other = jnp.take_along_axis(halves[h], low, axis=1, mode="promise_in_bounds")
            value = jnp.where(idx >= h * LANES, other, value)
        out.append(value)
    return out


def cross(a, b):
    return [
        a[1] * b[2] - a[2] * b[1],
        a[2] * b[0] - a[0] * b[2],
        a[0] * b[1] - a[1] * b[0],
    ]


def edges(verts, corner_ids):
    corners = [[pick_lanes(verts[d], corner_ids[k]) for d in range(3)] for k in range(3)]
    pieces = []
    for h in range(len(corner_ids[0])):
        a, b, c = [[corners[k][d][h] for d in range(3)] for k in range(3)]
        center = [(a[d] + b[d] + c[d]) * (1.0 / 3.0) for d in range(3)]
        one = [b[d] - a[d] for d in range(3)]
        two = [c[d] - a[d] for d in range(3)]
        normal = [0.5 * v for v in cross(one, two)]
        pieces.append((center, one, two, normal))
    return pieces


def root_norm(normal):
    return jnp.sqrt(normal[0] * normal[0] + normal[1] * normal[1] + normal[2] * normal[2] + AREA_SQ)


def kernel(
    cfg,
    x_hbm, tris_hbm, local_hbm, partner_hbm, ctrl_hbm, mom_hbm, tv_hbm, tt_hbm,
    tg_out, mg_hbm,
    x_ref, tris_ref, local_ref, partner_ref, ctrl_ref, mom, tv, tt, xs, xb, csc, khi, klo, khi_b, klo_b, bhi, blo, vel, own, tgt, mates, acc, geo, hot, cots, chi, mg, tgs,
    mom_sem, t_sem, xs_s, xs_r, pn_s, pn_r, ct_s, ct_r, tg_s, tg_r, out_sem,
):
    n, nsub, subjects, elems, ctrl, cdev, bits, chunk = cfg
    rows = 3 * subjects
    halves = elems // LANES
    groups = subjects // 8
    me = lax.axis_index("blk")
    sub = lax.axis_index("subj")

    loads = [
        pltpu.make_async_copy(x_hbm, x_ref, mom_sem.at[0]),
        pltpu.make_async_copy(ctrl_hbm, ctrl_ref, mom_sem.at[1]),
        pltpu.make_async_copy(mom_hbm, mom, mom_sem.at[2]),
    ]
    tloads = [
        pltpu.make_async_copy(tris_hbm, tris_ref, t_sem.at[0]),
        pltpu.make_async_copy(tv_hbm, tv, t_sem.at[1]),
        pltpu.make_async_copy(tt_hbm, tt, t_sem.at[2]),
        pltpu.make_async_copy(local_hbm, local_ref, t_sem.at[3]),
        pltpu.make_async_copy(partner_hbm, partner_ref, t_sem.at[4]),
    ]
    for c in loads + tloads:
        c.start()

    barrier = pltpu.get_barrier_semaphore()
    for o in range(1, n):
        pl.semaphore_signal(barrier, inc=1, device_id={"blk": me ^ o}, device_id_type=MESH)
    for o in range(1, nsub):
        pl.semaphore_signal(
            barrier, inc=1, device_id={"subj": lax.rem(sub + o, nsub)}, device_id_type=MESH
        )

    def spread(points, slot):
        padded = jnp.concatenate([points * SCALE, jnp.zeros((5, elems), f32)], axis=0)
        columns = padded.T
        for d in range(3):
            xb[slot, d] = jnp.broadcast_to(columns[:, d : d + 1], (elems, LANES))

    loads[0].wait()
    spread(x_ref[...], 0)
    loads[1].wait()
    csc[...] = ctrl_ref[...] * SCALE
    vel[...] = jnp.zeros_like(vel)

    def kernel_chunk(slot, start, hi_to, lo_to):
        cs = [csc[d : d + 1, pl.ds(start, chunk)] for d in range(3)]
        step = 32
        for r in range(0, elems, step):
            total = None
            for d in range(3):
                xv = xb[slot, d, pl.ds(r, step), :]
                off = jnp.concatenate([xv] * (chunk // LANES), axis=1) - cs[d]
                total = off * off if total is None else total + off * off
            hi, lo = split(jnp.exp2(-total))
            hi_to[pl.ds(r, step), :] = hi
            lo_to[pl.ds(r, step), :] = lo

    loads[2].wait()

    def weigh(start, hi_from, lo_from):
        m = mom[:, pl.ds(start, chunk)]
        weighted = [m]
        for d in range(3):
            weighted.append(m * ctrl_ref[d : d + 1, pl.ds(start, chunk)])
        pairs = [split(w) for w in weighted]
        hi = jnp.concatenate([p[0] for p in pairs], axis=0)
        both = mxu(jnp.concatenate([hi] + [p[1] for p in pairs], axis=0), hi_from[...], NT)
        vel[...] += both[0 : 4 * rows] + both[4 * rows :] + mxu(hi, lo_from[...], NT)

    at = lambda i: pl.multiple_of(i * chunk, chunk)
    steps = ctrl // chunk
    kernel_chunk(0, 0, khi, klo)

    def forward(i, carry):
        kernel_chunk(0, at(2 * i + 1), khi_b, klo_b)
        weigh(at(2 * i), khi, klo)
        kernel_chunk(0, at(jnp.minimum(2 * i + 2, steps - 1)), khi, klo)
        weigh(at(2 * i + 1), khi_b, klo_b)
        return carry

    lax.fori_loop(0, steps // 2, forward, 0)

    pl.semaphore_wait(barrier, n - 1 + nsub - 1)

    def to_blk(src, dst, ssem, rsem, o, s):
        return pltpu.make_async_remote_copy(
            src_ref=src, dst_ref=dst, send_sem=ssem.at[s], recv_sem=rsem.at[s],
            device_id={"blk": me ^ o}, device_id_type=MESH,
        )

    x_sends = [to_blk(x_ref, xs.at[o - 1], xs_s, xs_r, o, o - 1) for o in range(1, n)]
    for c in x_sends:
        c.start()

    tloads[0].wait()
    lane = lambda h: slice(h * LANES, (h + 1) * LANES)
    for g in range(groups):
        verts = [
            [
                x_ref[d : d + 1, lane(h)] + vel[pl.ds(d * subjects + g * 8, 8), lane(h)]
                for h in range(halves)
            ]
            for d in range(3)
        ]
        ids = [
            [jnp.broadcast_to(tris_ref[k : k + 1, lane(h)], (8, LANES)) for h in range(halves)]
            for k in range(3)
        ]
        for h, (center, one, two, normal) in enumerate(edges(verts, ids)):
            nu = root_norm(normal)
            inv = 1.0 / jnp.sqrt(nu)
            for d in range(3):
                own[d, g, h] = center[d] * SCALE
                own[3 + d, g, h] = normal[d] * inv
                geo[d, g, h] = one[d]
                geo[3 + d, g, h] = two[d]
                geo[6 + d, g, h] = normal[d]
            geo[9, g, h] = nu

    p_sends = [to_blk(own, mates.at[b], pn_s, pn_r, 2**b, b) for b in range(bits)]
    for c in p_sends:
        c.start()

    for c in tloads[1:]:
        c.wait()
    for g in range(groups):
        part = lambda d: pl.ds(d * subjects + g * 8, 8)
        verts = [[tv[part(d), lane(h)] for h in range(halves)] for d in range(3)]
        ids = [[tt[part(k), lane(h)] for h in range(halves)] for k in range(3)]
        for h, (center, one, two, normal) in enumerate(edges(verts, ids)):
            inv = 1.0 / jnp.sqrt(root_norm(normal))
            for d in range(3):
                tgt[d, g, h] = center[d] * SCALE
                tgt[3 + d, g, h] = normal[d] * inv

    for k in range(3):
        vertex = lax.broadcasted_iota(jnp.int32, (elems, elems), 0)
        hot[:, k * elems : (k + 1) * elems] = jnp.where(
            vertex == tris_ref[k : k + 1, :], 1.0, 0.0
        ).astype(bf16)

    acc[...] = jnp.zeros_like(acc)

    def interact(q, g, a_blocks, coefs):
        p = [[own[d, g, a] for d in range(3)] for a in a_blocks]
        u = [[geo[6 + d, g, a] for d in range(3)] for a in a_blocks]
        unroll = UNROLL

        def body(i, sums):
            sums = list(sums)
            for v in range(unroll):
                shift = v if unroll == LANES else i * unroll + v
                rolled = [pltpu.roll(value, shift, 1) if v or unroll < LANES else value for value in q]
                for x in range(len(a_blocks)):
                    off = [p[x][d] - rolled[d] for d in range(3)]
                    weight = jnp.exp2(-(off[0] * off[0] + off[1] * off[1] + off[2] * off[2]))
                    inner = (
                        u[x][0] * rolled[3] + u[x][1] * rolled[4] + u[x][2] * rolled[5]
                    )
                    t = weight * inner
                    s = t * inner
                    for d in range(3):
                        sums[6 * x + d] = sums[6 * x + d] + s * off[d]
                        sums[6 * x + 3 + d] = sums[6 * x + 3 + d] + t * rolled[3 + d]
            return tuple(sums)

        sums = (jnp.zeros((8, LANES), f32),) * (6 * len(a_blocks))
        if unroll == LANES:
            sums = body(0, sums)
        else:
            sums = lax.fori_loop(0, LANES // unroll, body, sums)
        for x, a in enumerate(a_blocks):
            for d in range(6):
                acc[d, g, a] += coefs[x] * sums[6 * x + d]

    every = list(range(halves))
    as_float = lambda v: v.astype(f32)

    def near_target(i, carry):
        b, g = i // groups, i % groups
        interact([tgt[d, g, b] for d in range(6)], g, [b], [-2.0])
        return carry

    def near_own(i, carry):
        b, g = i // groups, i % groups
        local = [as_float(local_ref[a, b] + local_ref[b, a]) for a in every]
        interact([own[d, g, b] for d in range(6)], g, every, local)
        return carry

    lax.fori_loop(0, halves * groups, near_target, 0)
    lax.fori_loop(0, halves * groups, near_own, 0)

    for bit in range(bits):
        p_sends[bit].wait_recv()

        def far(i, carry, bit=bit):
            b, g = i // groups, i % groups
            coefs = []
            for a in every:
                count = jnp.int32(0)
                for r in range(4):
                    if r % (n.bit_length() - 1) == bit:
                        count = count + jnp.where(partner_ref[a, r] == b, 2, 0)
                coefs.append(as_float(count))
            interact([mates[bit, d, g, b] for d in range(6)], g, every, coefs)
            return carry

        lax.fori_loop(0, halves * groups, far, 0)

    width = 1.0 / LANES
    corner = [[[[None] * halves for _ in range(groups)] for _ in range(3)] for _ in range(3)]
    for g in range(groups):
        for h in range(halves):
            one = [geo[d, g, h] for d in range(3)]
            two = [geo[3 + d, g, h] for d in range(3)]
            u = [geo[6 + d, g, h] for d in range(3)]
            inv = 1.0 / geo[9, g, h]
            moved = [acc[d, g, h] for d in range(3)]
            turned = [acc[3 + d, g, h] for d in range(3)]
            total = u[0] * turned[0] + u[1] * turned[1] + u[2] * turned[2]
            shrink = inv * inv * inv * total
            gp = [moved[d] * inv * (-2.0 * width / SCALE / 3.0) for d in range(3)]
            gu = [(2.0 * inv * turned[d] - u[d] * shrink) * (0.5 * width) for d in range(3)]
            g_one = cross(two, gu)
            g_two = cross(gu, one)
            for d in range(3):
                corner[0][d][g][h] = gp[d] - g_one[d] - g_two[d]
                corner[1][d][g][h] = gp[d] + g_one[d]
                corner[2][d][g][h] = gp[d] + g_two[d]
    for k in range(3):
        for h in range(halves):
            column = pl.ds(k * elems + h * LANES, LANES)
            value = jnp.concatenate(
                [corner[k][d][g][h] for d in range(3) for g in range(groups)], axis=0
            )
            hi, lo = split(value)
            chi[0:rows, column] = hi
            chi[rows : 2 * rows, column] = lo
    both = mxu(chi[...], hot[...], NT)
    cot = both[0:rows] + both[rows : 2 * rows]
    cots[0] = cot

    c_sends = [to_blk(cots.at[0], cots.at[o], ct_s, ct_r, o, o - 1) for o in range(1, n)]
    for c in c_sends:
        c.start()

    def over_rows(value):
        return jnp.sum(value, axis=0, keepdims=True)

    plain = over_rows(cot * vel[0:rows, :])
    factor = 1.0 / (subjects * nsub)
    for d in range(3):
        direct = over_rows(cot[d * subjects : (d + 1) * subjects])
        moved = over_rows(cot * vel[(d + 1) * rows : (d + 2) * rows, :])
        tgs[sub, pl.ds(d, 1), :] = factor * (direct - 2.0 * (x_ref[d : d + 1, :] * plain - moved))

    g_sends = []
    for o in range(1, nsub):
        g_sends.append(
            pltpu.make_async_remote_copy(
                src_ref=tgs.at[sub], dst_ref=tgs.at[sub], send_sem=tg_s.at[o - 1],
                recv_sem=tg_r.at[o - 1], device_id={"subj": lax.rem(sub + o, nsub)},
                device_id_type=MESH,
            )
        )
    for c in g_sends:
        c.start()

    for o in range(1, n):
        x_sends[o - 1].wait_recv()
        spread(xs[o - 1], o)

    def backward(make, use):
        if use is not None:
            hi, lo = split(cots[use])
            two = jnp.concatenate([hi, lo], axis=0)

        def body(i, carry):
            here = pl.ds(at(i), chunk)
            if make is not None:
                start = pl.multiple_of(me * cdev + i * chunk, chunk)
                kernel_chunk(make, start, bhi.at[make, :, here], blo.at[make, :, here])
            if use is not None:
                both = mxu(two, bhi[use, :, here], NN)
                term = both[0:rows] + both[rows:] + mxu(hi, blo[use, :, here], NN)
                mg[:, here] = mg[:, here] + term if use else term
            return carry

        lax.fori_loop(0, cdev // chunk, body, 0)

    backward(0, None)
    backward(1, 0)
    if n > 2:
        backward(2, None)
    for o in range(1, n):
        c_sends[o - 1].wait_recv()
        backward(o + 2 if o + 2 < n else None, o)

    outs = [pltpu.make_async_copy(mg, mg_hbm, out_sem.at[0])]
    for c in outs:
        c.start()
    for c in g_sends:
        c.wait_recv()
    tg_sum = tgs[0]
    for o in range(1, nsub):
        tg_sum = tg_sum + tgs[o]
    tg_out[...] = tg_sum
    for c in x_sends + p_sends + c_sends + g_sends:
        c.wait_send()
    for c in outs:
        c.wait()


def on_device(n, nsub, tverts, ttris, local, partner, controls, momenta, tv, tt):
    subjects, _, ctrl = momenta.shape
    elems = tverts.shape[1]
    halves = elems // LANES
    groups = subjects // 8
    rows = 3 * subjects
    cdev = ctrl // n
    bits = min(4, n.bit_length() - 1)
    chunk = min(512, cdev)
    cfg = (n, nsub, subjects, elems, ctrl, cdev, bits, chunk)
    vmem = pl.BlockSpec(memory_space=pltpu.VMEM)
    hbm = pl.BlockSpec(memory_space=pltpu.HBM)
    panel = (6, groups, halves, 8, LANES)
    dma = pltpu.SemaphoreType.DMA
    by_axis = lambda v: v.transpose(1, 0, 2).reshape(rows, v.shape[2])
    template_grad, grads = pl.pallas_call(
        functools.partial(kernel, cfg),
        out_shape=(
            jax.ShapeDtypeStruct((3, elems), f32),
            jax.ShapeDtypeStruct((rows, cdev), f32),
        ),
        in_specs=[hbm] * 8,
        out_specs=(vmem, hbm),
        scratch_shapes=[
            pltpu.VMEM((3, elems), f32),
            pltpu.VMEM((3, elems), jnp.int32),
            pltpu.SMEM(local.shape, jnp.int32),
            pltpu.SMEM(partner.shape[::-1], jnp.int32),
            pltpu.VMEM((3, ctrl), f32),
            pltpu.VMEM((rows, ctrl), f32),
            pltpu.VMEM((rows, elems), f32),
            pltpu.VMEM((rows, elems), jnp.int32),
            pltpu.VMEM((n - 1, 3, elems), f32),
            pltpu.VMEM((n, 3, elems, LANES), f32),
            pltpu.VMEM((3, ctrl), f32),
            pltpu.VMEM((elems, chunk), bf16),
            pltpu.VMEM((elems, chunk), bf16),
            pltpu.VMEM((elems, chunk), bf16),
            pltpu.VMEM((elems, chunk), bf16),
            pltpu.VMEM((n, elems, cdev), bf16),
            pltpu.VMEM((n, elems, cdev), bf16),
            pltpu.VMEM((4 * rows, elems), f32),
            pltpu.VMEM(panel, f32),
            pltpu.VMEM(panel, f32),
            pltpu.VMEM((bits,) + panel, f32),
            pltpu.VMEM(panel, f32),
            pltpu.VMEM((10,) + panel[1:], f32),
            pltpu.VMEM((elems, 3 * elems), bf16),
            pltpu.VMEM((n, rows, elems), f32),
            pltpu.VMEM((2 * rows, 3 * elems), bf16),
            pltpu.VMEM((rows, cdev), f32),
            pltpu.VMEM((nsub, 3, elems), f32),
            dma((3,)), dma((5,)),
            dma((n - 1,)), dma((n - 1,)),
            dma((bits,)), dma((bits,)),
            dma((n - 1,)), dma((n - 1,)),
            dma((nsub - 1,)), dma((nsub - 1,)),
            dma((1,)),
        ],
        compiler_params=pltpu.CompilerParams(
            collective_id=0, has_side_effects=True, vmem_limit_bytes=64 * 2**20
        ),
        name="atlas",
    )(tverts, ttris, local, partner.T, controls, by_axis(momenta), by_axis(tv), by_axis(tt))
    return template_grad, grads.reshape(3, subjects, cdev).transpose(1, 0, 2)


def solution(mesh):
    return jax.shard_map(
        functools.partial(on_device, mesh.shape["blk"], mesh.shape["subj"]),
        mesh=mesh,
        in_specs=(
            P(None, ("groups", "blk")),
            P(None, ("groups", "blk")),
            P("blk", None),
            P(None, "blk"),
            P(),
            P(("groups", "subj"), None, None),
            P(("groups", "subj"), None, "blk"),
            P(("groups", "subj"), None, "blk"),
        ),
        out_specs=(P(None, ("groups", "blk")), P(("groups", "subj"), None, "blk")),
        check_vma=False,
    )
```

```python
import functools
import math

import jax
import jax.numpy as jnp
from jax import lax
from jax.experimental import pallas as pl
from jax.experimental.pallas import tpu as pltpu
from jax.sharding import PartitionSpec as P

AREA_SQ = 0.25
SCALE = math.sqrt(math.log2(math.e))
LANES = 128
UNROLL = 128
MESH = pl.DeviceIdType.MESH
f32, bf16 = jnp.float32, jnp.bfloat16
NT = (((1,), (1,)), ((), ()))
NN = (((1,), (0,)), ((), ()))


def split(value):
    high = value.astype(bf16)
    return high, (value - high.astype(f32)).astype(bf16)


def mxu(a, b, dims):
    return lax.dot_general(a, b, dims, preferred_element_type=f32)


def pick_lanes(halves, indices):
    out = []
    for idx in indices:
        low = idx & (LANES - 1)
        value = jnp.take_along_axis(halves[0], low, axis=1, mode="promise_in_bounds")
        for h in range(1, len(halves)):
            other = jnp.take_along_axis(halves[h], low, axis=1, mode="promise_in_bounds")
            value = jnp.where(idx >= h * LANES, other, value)
        out.append(value)
    return out


def cross(a, b):
    return [
        a[1] * b[2] - a[2] * b[1],
        a[2] * b[0] - a[0] * b[2],
        a[0] * b[1] - a[1] * b[0],
    ]


def edges(verts, corner_ids):
    corners = [[pick_lanes(verts[d], corner_ids[k]) for d in range(3)] for k in range(3)]
    pieces = []
    for h in range(len(corner_ids[0])):
        a, b, c = [[corners[k][d][h] for d in range(3)] for k in range(3)]
        center = [(a[d] + b[d] + c[d]) * (1.0 / 3.0) for d in range(3)]
        one = [b[d] - a[d] for d in range(3)]
        two = [c[d] - a[d] for d in range(3)]
        normal = [0.5 * v for v in cross(one, two)]
        pieces.append((center, one, two, normal))
    return pieces


def root_norm(normal):
    return jnp.sqrt(normal[0] * normal[0] + normal[1] * normal[1] + normal[2] * normal[2] + AREA_SQ)


def kernel(
    cfg,
    x_hbm, tris_hbm, local_hbm, partner_hbm, ctrl_hbm, mom_hbm, tv_hbm, tt_hbm,
    tg_out, mg_hbm,
    x_ref, tris_ref, local_ref, partner_ref, ctrl_ref, mom, tv, tt, xs, xb, csc, khi, klo, khi_b, klo_b, bhi, blo, vel, own, tgt, mates, acc, geo, hot, cots, chi, mg, tgs,
    mom_sem, t_sem, xs_s, xs_r, pn_s, pn_r, ct_s, ct_r, tg_s, tg_r, out_sem,
):
    n, nsub, subjects, elems, ctrl, cdev, bits, chunk = cfg
    rows = 3 * subjects
    halves = elems // LANES
    groups = subjects // 8
    me = lax.axis_index("blk")
    sub = lax.axis_index("subj")

    loads = [
        pltpu.make_async_copy(x_hbm, x_ref, mom_sem.at[0]),
        pltpu.make_async_copy(ctrl_hbm, ctrl_ref, mom_sem.at[1]),
        pltpu.make_async_copy(mom_hbm, mom, mom_sem.at[2]),
    ]
    tloads = [
        pltpu.make_async_copy(tris_hbm, tris_ref, t_sem.at[0]),
        pltpu.make_async_copy(tv_hbm, tv, t_sem.at[1]),
        pltpu.make_async_copy(tt_hbm, tt, t_sem.at[2]),
        pltpu.make_async_copy(local_hbm, local_ref, t_sem.at[3]),
        pltpu.make_async_copy(partner_hbm, partner_ref, t_sem.at[4]),
    ]
    for c in loads + tloads:
        c.start()

    barrier = pltpu.get_barrier_semaphore()
    for o in range(1, n):
        pl.semaphore_signal(barrier, inc=1, device_id={"blk": me ^ o}, device_id_type=MESH)
    for o in range(1, nsub):
        pl.semaphore_signal(
            barrier, inc=1, device_id={"subj": lax.rem(sub + o, nsub)}, device_id_type=MESH
        )

    def spread(points, slot):
        padded = jnp.concatenate([points * SCALE, jnp.zeros((5, elems), f32)], axis=0)
        columns = padded.T
        for d in range(3):
            xb[slot, d] = jnp.broadcast_to(columns[:, d : d + 1], (elems, LANES))

    loads[0].wait()
    spread(x_ref[...], 0)
    loads[1].wait()
    csc[...] = ctrl_ref[...] * SCALE
    vel[...] = jnp.zeros_like(vel)

    def kernel_chunk(slot, start, hi_to, lo_to):
        cs = [csc[d : d + 1, pl.ds(start, chunk)] for d in range(3)]
        step = 32
        for r in range(0, elems, step):
            total = None
            for d in range(3):
                xv = xb[slot, d, pl.ds(r, step), :]
                off = jnp.concatenate([xv] * (chunk // LANES), axis=1) - cs[d]
                total = off * off if total is None else total + off * off
            hi, lo = split(jnp.exp2(-total))
            hi_to[pl.ds(r, step), :] = hi
            lo_to[pl.ds(r, step), :] = lo

    loads[2].wait()

    def weigh(start, hi_from, lo_from):
        m = mom[:, pl.ds(start, chunk)]
        weighted = [m]
        for d in range(3):
            weighted.append(m * ctrl_ref[d : d + 1, pl.ds(start, chunk)])
        pairs = [split(w) for w in weighted]
        hi = jnp.concatenate([p[0] for p in pairs], axis=0)
        both = mxu(jnp.concatenate([hi] + [p[1] for p in pairs], axis=0), hi_from[...], NT)
        vel[...] += both[0 : 4 * rows] + both[4 * rows :] + mxu(hi, lo_from[...], NT)

    at = lambda i: pl.multiple_of(i * chunk, chunk)
    steps = ctrl // chunk
    kernel_chunk(0, 0, khi, klo)

    def forward(i, carry):
        kernel_chunk(0, at(2 * i + 1), khi_b, klo_b)
        weigh(at(2 * i), khi, klo)
        kernel_chunk(0, at(jnp.minimum(2 * i + 2, steps - 1)), khi, klo)
        weigh(at(2 * i + 1), khi_b, klo_b)
        return carry

    lax.fori_loop(0, steps // 2, forward, 0)

    pl.semaphore_wait(barrier, n - 1 + nsub - 1)

    def to_blk(src, dst, ssem, rsem, o, s):
        return pltpu.make_async_remote_copy(
            src_ref=src, dst_ref=dst, send_sem=ssem.at[s], recv_sem=rsem.at[s],
            device_id={"blk": me ^ o}, device_id_type=MESH,
        )

    x_sends = [to_blk(x_ref, xs.at[o - 1], xs_s, xs_r, o, o - 1) for o in range(1, n)]
    for c in x_sends:
        c.start()

    tloads[0].wait()
    lane = lambda h: slice(h * LANES, (h + 1) * LANES)
    for g in range(groups):
        verts = [
            [
                x_ref[d : d + 1, lane(h)] + vel[pl.ds(d * subjects + g * 8, 8), lane(h)]
                for h in range(halves)
            ]
            for d in range(3)
        ]
        ids = [
            [jnp.broadcast_to(tris_ref[k : k + 1, lane(h)], (8, LANES)) for h in range(halves)]
            for k in range(3)
        ]
        for h, (center, one, two, normal) in enumerate(edges(verts, ids)):
            nu = root_norm(normal)
            inv = 1.0 / jnp.sqrt(nu)
            for d in range(3):
                own[d, g, h] = center[d] * SCALE
                own[3 + d, g, h] = normal[d] * inv
                geo[d, g, h] = one[d]
                geo[3 + d, g, h] = two[d]
                geo[6 + d, g, h] = normal[d]
            geo[9, g, h] = nu

    p_sends = [to_blk(own, mates.at[b], pn_s, pn_r, 2**b, b) for b in range(bits)]
    for c in p_sends:
        c.start()

    for c in tloads[1:]:
        c.wait()
    for g in range(groups):
        part = lambda d: pl.ds(d * subjects + g * 8, 8)
        verts = [[tv[part(d), lane(h)] for h in range(halves)] for d in range(3)]
        ids = [[tt[part(k), lane(h)] for h in range(halves)] for k in range(3)]
        for h, (center, one, two, normal) in enumerate(edges(verts, ids)):
            inv = 1.0 / jnp.sqrt(root_norm(normal))
            for d in range(3):
                tgt[d, g, h] = center[d] * SCALE
                tgt[3 + d, g, h] = normal[d] * inv

    for k in range(3):
        vertex = lax.broadcasted_iota(jnp.int32, (elems, elems), 0)
        hot[:, k * elems : (k + 1) * elems] = jnp.where(
            vertex == tris_ref[k : k + 1, :], 1.0, 0.0
        ).astype(bf16)

    acc[...] = jnp.zeros_like(acc)

    def interact(q, g, a_blocks, coefs):
        p = [[own[d, g, a] for d in range(3)] for a in a_blocks]
        u = [[geo[6 + d, g, a] for d in range(3)] for a in a_blocks]
        unroll = UNROLL

        def body(i, sums):
            sums = list(sums)
            for v in range(unroll):
                shift = v if unroll == LANES else i * unroll + v
                rolled = [pltpu.roll(value, shift, 1) if v or unroll < LANES else value for value in q]
                for x in range(len(a_blocks)):
                    off = [p[x][d] - rolled[d] for d in range(3)]
                    weight = jnp.exp2(-(off[0] * off[0] + off[1] * off[1] + off[2] * off[2]))
                    inner = (
                        u[x][0] * rolled[3] + u[x][1] * rolled[4] + u[x][2] * rolled[5]
                    )
                    t = weight * inner
                    s = t * inner
                    for d in range(3):
                        sums[6 * x + d] = sums[6 * x + d] + s * off[d]
                        sums[6 * x + 3 + d] = sums[6 * x + 3 + d] + t * rolled[3 + d]
            return tuple(sums)

        sums = (jnp.zeros((8, LANES), f32),) * (6 * len(a_blocks))
        if unroll == LANES:
            sums = body(0, sums)
        else:
            sums = lax.fori_loop(0, LANES // unroll, body, sums)
        for x, a in enumerate(a_blocks):
            for d in range(6):
                acc[d, g, a] += coefs[x] * sums[6 * x + d]

    every = list(range(halves))
    as_float = lambda v: v.astype(f32)

    def near_target(i, carry):
        b, g = i // groups, i % groups
        interact([tgt[d, g, b] for d in range(6)], g, [b], [-2.0])
        return carry

    def near_own(i, carry):
        b, g = i // groups, i % groups
        local = [as_float(local_ref[a, b] + local_ref[b, a]) for a in every]
        interact([own[d, g, b] for d in range(6)], g, every, local)
        return carry

    lax.fori_loop(0, halves * groups, near_target, 0)
    lax.fori_loop(0, halves * groups, near_own, 0)

    for bit in range(bits):
        p_sends[bit].wait_recv()

        def far(i, carry, bit=bit):
            b, g = i // groups, i % groups
            coefs = []
            for a in every:
                count = jnp.int32(0)
                for r in range(4):
                    if r % (n.bit_length() - 1) == bit:
                        count = count + jnp.where(partner_ref[a, r] == b, 2, 0)
                coefs.append(as_float(count))
            interact([mates[bit, d, g, b] for d in range(6)], g, every, coefs)
            return carry

        lax.fori_loop(0, halves * groups, far, 0)

    width = 1.0 / LANES
    corner = [[[[None] * halves for _ in range(groups)] for _ in range(3)] for _ in range(3)]
    for g in range(groups):
        for h in range(halves):
            one = [geo[d, g, h] for d in range(3)]
            two = [geo[3 + d, g, h] for d in range(3)]
            u = [geo[6 + d, g, h] for d in range(3)]
            inv = 1.0 / geo[9, g, h]
            moved = [acc[d, g, h] for d in range(3)]
            turned = [acc[3 + d, g, h] for d in range(3)]
            total = u[0] * turned[0] + u[1] * turned[1] + u[2] * turned[2]
            shrink = inv * inv * inv * total
            gp = [moved[d] * inv * (-2.0 * width / SCALE / 3.0) for d in range(3)]
            gu = [(2.0 * inv * turned[d] - u[d] * shrink) * (0.5 * width) for d in range(3)]
            g_one = cross(two, gu)
            g_two = cross(gu, one)
            for d in range(3):
                corner[0][d][g][h] = gp[d] - g_one[d] - g_two[d]
                corner[1][d][g][h] = gp[d] + g_one[d]
                corner[2][d][g][h] = gp[d] + g_two[d]
    for k in range(3):
        for h in range(halves):
            column = pl.ds(k * elems + h * LANES, LANES)
            value = jnp.concatenate(
                [corner[k][d][g][h] for d in range(3) for g in range(groups)], axis=0
            )
            hi, lo = split(value)
            chi[0:rows, column] = hi
            chi[rows : 2 * rows, column] = lo
    both = mxu(chi[...], hot[...], NT)
    cot = both[0:rows] + both[rows : 2 * rows]
    cots[0] = cot

    c_sends = [to_blk(cots.at[0], cots.at[o], ct_s, ct_r, o, o - 1) for o in range(1, n)]
    for c in c_sends:
        c.start()

    def over_rows(value):
        return jnp.sum(value, axis=0, keepdims=True)

    plain = over_rows(cot * vel[0:rows, :])
    factor = 1.0 / (subjects * nsub)
    for d in range(3):
        direct = over_rows(cot[d * subjects : (d + 1) * subjects])
        moved = over_rows(cot * vel[(d + 1) * rows : (d + 2) * rows, :])
        tgs[sub, pl.ds(d, 1), :] = factor * (direct - 2.0 * (x_ref[d : d + 1, :] * plain - moved))

    g_sends = []
    for o in range(1, nsub):
        g_sends.append(
            pltpu.make_async_remote_copy(
                src_ref=tgs.at[sub], dst_ref=tgs.at[sub], send_sem=tg_s.at[o - 1],
                recv_sem=tg_r.at[o - 1], device_id={"subj": lax.rem(sub + o, nsub)},
                device_id_type=MESH,
            )
        )
    for c in g_sends:
        c.start()

    for o in range(1, n):
        x_sends[o - 1].wait_recv()
        spread(xs[o - 1], o)

    def backward(make, use):
        if use is not None:
            hi, lo = split(cots[use])
            two = jnp.concatenate([hi, lo], axis=0)

        def body(i, carry):
            here = pl.ds(at(i), chunk)
            if make is not None:
                start = pl.multiple_of(me * cdev + i * chunk, chunk)
                kernel_chunk(make, start, bhi.at[make, :, here], blo.at[make, :, here])
            if use is not None:
                both = mxu(two, bhi[use, :, here], NN)
                term = both[0:rows] + both[rows:] + mxu(hi, blo[use, :, here], NN)
                mg[:, here] = mg[:, here] + term if use else term
            return carry

        lax.fori_loop(0, cdev // chunk, body, 0)

    backward(0, None)
    backward(1, 0)
    if n > 2:
        backward(2, None)
    for o in range(1, n):
        c_sends[o - 1].wait_recv()
        backward(o + 2 if o + 2 < n else None, o)

    outs = [pltpu.make_async_copy(mg, mg_hbm, out_sem.at[0])]
    for c in outs:
        c.start()
    for c in g_sends:
        c.wait_recv()
    tg_sum = tgs[0]
    for o in range(1, nsub):
        tg_sum = tg_sum + tgs[o]
    tg_out[...] = tg_sum
    for c in x_sends + p_sends + c_sends + g_sends:
        c.wait_send()
    for c in outs:
        c.wait()


def on_device(n, nsub, tverts, ttris, local, partner, controls, momenta, tv, tt):
    subjects, _, ctrl = momenta.shape
    elems = tverts.shape[1]
    halves = elems // LANES
    groups = subjects // 8
    rows = 3 * subjects
    cdev = ctrl // n
    bits = min(4, n.bit_length() - 1)
    chunk = min(512, cdev)
    cfg = (n, nsub, subjects, elems, ctrl, cdev, bits, chunk)
    vmem = pl.BlockSpec(memory_space=pltpu.VMEM)
    hbm = pl.BlockSpec(memory_space=pltpu.HBM)
    panel = (6, groups, halves, 8, LANES)
    dma = pltpu.SemaphoreType.DMA
    by_axis = lambda v: v.transpose(1, 0, 2).reshape(rows, v.shape[2])
    template_grad, grads = pl.pallas_call(
        functools.partial(kernel, cfg),
        out_shape=(
            jax.ShapeDtypeStruct((3, elems), f32),
            jax.ShapeDtypeStruct((rows, cdev), f32),
        ),
        in_specs=[hbm] * 8,
        out_specs=(vmem, hbm),
        scratch_shapes=[
            pltpu.VMEM((3, elems), f32),
            pltpu.VMEM((3, elems), jnp.int32),
            pltpu.SMEM(local.shape, jnp.int32),
            pltpu.SMEM(partner.shape[::-1], jnp.int32),
            pltpu.VMEM((3, ctrl), f32),
            pltpu.VMEM((rows, ctrl), f32),
            pltpu.VMEM((rows, elems), f32),
            pltpu.VMEM((rows, elems), jnp.int32),
            pltpu.VMEM((n - 1, 3, elems), f32),
            pltpu.VMEM((n, 3, elems, LANES), f32),
            pltpu.VMEM((3, ctrl), f32),
            pltpu.VMEM((elems, chunk), bf16),
            pltpu.VMEM((elems, chunk), bf16),
            pltpu.VMEM((elems, chunk), bf16),
            pltpu.VMEM((elems, chunk), bf16),
            pltpu.VMEM((n, elems, cdev), bf16),
            pltpu.VMEM((n, elems, cdev), bf16),
            pltpu.VMEM((4 * rows, elems), f32),
            pltpu.VMEM(panel, f32),
            pltpu.VMEM(panel, f32),
            pltpu.VMEM((bits,) + panel, f32),
            pltpu.VMEM(panel, f32),
            pltpu.VMEM((10,) + panel[1:], f32),
            pltpu.VMEM((elems, 3 * elems), bf16),
            pltpu.VMEM((n, rows, elems), f32),
            pltpu.VMEM((2 * rows, 3 * elems), bf16),
            pltpu.VMEM((rows, cdev), f32),
            pltpu.VMEM((nsub, 3, elems), f32),
            dma((3,)), dma((5,)),
            dma((n - 1,)), dma((n - 1,)),
            dma((bits,)), dma((bits,)),
            dma((n - 1,)), dma((n - 1,)),
            dma((nsub - 1,)), dma((nsub - 1,)),
            dma((1,)),
        ],
        compiler_params=pltpu.CompilerParams(
            collective_id=0, has_side_effects=True, vmem_limit_bytes=64 * 2**20
        ),
        name="atlas",
    )(tverts, ttris, local, partner.T, controls, by_axis(momenta), by_axis(tv), by_axis(tt))
    return template_grad, grads.reshape(3, subjects, cdev).transpose(1, 0, 2)


def solution(mesh):
    return jax.shard_map(
        functools.partial(on_device, mesh.shape["blk"], mesh.shape["subj"]),
        mesh=mesh,
        in_specs=(
            P(None, ("groups", "blk")),
            P(None, ("groups", "blk")),
            P("blk", None),
            P(None, "blk"),
            P(),
            P(("groups", "subj"), None, None),
            P(("groups", "subj"), None, "blk"),
            P(("groups", "subj"), None, "blk"),
        ),
        out_specs=(P(None, ("groups", "blk")), P(("groups", "subj"), None, "blk")),
        check_vma=False,
    )
```
